512 devices in a mesh: lat: 16 (over x, y_lo), lon: 32 (over z, y_hi, core).
Axes of the slice: x: 4, y: 8 (y_hi: 2, y_lo: 4; y = y_hi * 4 + y_lo), z: 8, core: 2. Of those that a mesh axis runs over, the one named last changes fastest.
Arguments:
- ensemble: float32 [64, 256, 1792], P('lat', 'lon'), may hold values from -6 to 6
- northward_wind: float32 [64, 256], P('lat', 'lon'), may hold values from -1 to 1
- eastward_wind: float32 [64, 256], P('lat', 'lon'), may hold values from -1 to 1
- spreading_strength: float32 [64, 256], P('lat', 'lon'), may hold values from 0.05 to 0.2
- measurement_home_subdomain: int32 [3, 512], replicated, may hold values from 0 to 511, as said below
- obs_site: int32 [3, 512], replicated, may hold values from 0 to 895
- obs_class: int32 [3, 512], replicated, may hold values from 0 to 7
- cutoff_table: int32 [8], replicated, may hold values from 6 to 23
- obs_value: float32 [3, 512], replicated, may hold values from -6 to 6
- obs_var: float32 [3, 512], replicated, may hold values from 0.5 to 2
- obs_noise: float32 [3, 512, 64], replicated, may hold values from -6 to 6
Outputs:
- analysis: float32 [64, 256, 1792], P('lat', 'lon')
The draws below stay inside these ranges and needn't reach their ends.
Inputs may be any that keep to these rules, and one draw needn't show every extreme that they name: `measurement_home_subdomain`: tile index is lat index * 32 + lon index; in every batch no tile owns more than 4 observations and some tile owns exactly 4.
All inputs are finite; a program needn't handle non-finite values.
Results may differ from the reference program's by a relative error of at most 0.0003.
Values sent between devices are 32-bit elements; how exact they have to be, the bound alone decides.
No kernel may reach another device: no remote copies, remote signals or barrier semaphores. Data moves between devices by JAX's collectives and lax.ppermute only.
A program may use at most 64 MiB of HBM per device.

```python
import math
import jax
import jax.numpy as jnp
from jax import lax

CLAT = 4
CLON = 8
LEV = 28
MEMBERS = 64
SECTIONS = 2
BATCH_GROUPS = 3
CAP = 4
CLASSES = 8
NB = 512
NLAT = 64
NLON = 256
CELLS = 32
N_LAT = 16
N_LON = 32


def draw_measurement_home_subdomain(key, part):
    tiles = N_LAT * N_LON
    batches = []
    for b in range(BATCH_GROUPS):
        sub = jax.random.fold_in(key, b + 11)
        order_tiles = jax.random.permutation(jax.random.fold_in(sub, 1), tiles).astype(jnp.int32)
        hot = order_tiles[tiles - 1]
        rest = order_tiles[jnp.arange(NB - CAP, dtype=jnp.int32) % (tiles - 1)]
        listed = jnp.concatenate([jnp.full((CAP,), hot, jnp.int32), rest])
        shuffle_order = jax.random.permutation(jax.random.fold_in(sub, 2), NB).astype(jnp.int32)
        batches.append(listed[shuffle_order])
    return jnp.stack(batches).astype(jnp.int32)


def with_ends(drawn, stream_key, smallest, largest):
    extent = drawn.shape
    index_at = [jax.random.randint(jax.random.fold_in(stream_key, axis), (), 0, extent[axis]) for axis in range(len(extent))]
    drawn = drawn.at[tuple(index_at)].set(smallest)
    longest = extent.index(max(extent))
    index_at[longest] = (index_at[longest] + 1) % extent[longest]
    return drawn.at[tuple(index_at)].set(largest)


def block_scale(rng, dims, cuts, smallest, largest):
    factor_of, own = 1.0, jax.random.fold_in(rng, 6)
    for dim, parts in cuts:
        draws = jnp.exp(jax.random.uniform(jax.random.fold_in(own, dim), (parts,), jnp.float32, smallest / len(cuts), largest / len(cuts)))
        factor_of = factor_of * jnp.repeat(draws, dims[dim] // parts).reshape([-1 if axis == dim else 1 for axis in range(len(dims))])
    return factor_of


def centred(key, dims, width, reach, pieces=(), kind=jnp.bfloat16):
    array = width * jax.random.normal(key, dims, jnp.float32)
    if pieces:
        array = array * block_scale(key, dims, pieces, -0.22, 0.18)
    return jnp.clip(array, -reach, reach).astype(kind)


def setup_inputs(seed: int = 0) -> dict:
    key_list = jax.random.split(jax.random.key(seed), 12)
    ensemble = centred(key_list[0], (NLAT, NLON, LEV * MEMBERS), 1.0, 6.0, ((0, 16), (1, 32)), jnp.float32)
    northward_wind = jnp.clip(jax.random.uniform(key_list[1], (NLAT, NLON), jnp.float32, -1.0, 1.0) * block_scale(key_list[1], (NLAT, NLON), ((0, 16), (1, 32)), -0.4, 0.0), -1.0, 1.0)
    eastward_wind = jnp.clip(jax.random.uniform(key_list[2], (NLAT, NLON), jnp.float32, -1.0, 1.0) * block_scale(key_list[2], (NLAT, NLON), ((0, 16), (1, 32)), -0.4, 0.0), -1.0, 1.0)
    spreading_strength = jnp.clip(jnp.exp(math.log(0.2) - 1.3862944 * jax.random.uniform(key_list[3], (NLAT, NLON), jnp.float32) ** block_scale(key_list[3], (NLAT, NLON), ((0, 16), (1, 32)), -0.2, 0.2)), 0.05, 0.2)
    measurement_home_subdomain = draw_measurement_home_subdomain(jax.random.fold_in(key_list[11], 71), 0)
    obs_site = with_ends(jax.random.randint(key_list[5], (BATCH_GROUPS, NB), 0, CELLS * LEV), jax.random.fold_in(key_list[5], 1), 0, (CELLS * LEV) - 1).astype(jnp.int32)
    obs_class = with_ends(jax.random.randint(key_list[6], (BATCH_GROUPS, NB), 0, CLASSES), jax.random.fold_in(key_list[6], 1), 0, CLASSES - 1).astype(jnp.int32)
    cutoff_table = with_ends(jax.random.randint(key_list[7], (CLASSES,), 6, 24), jax.random.fold_in(key_list[7], 1), 6, 23).astype(jnp.int32)
    obs_value = centred(key_list[8], (BATCH_GROUPS, NB), 1.0, 6.0, (), jnp.float32)
    obs_var = jnp.clip(jnp.exp(jax.random.uniform(key_list[9], (BATCH_GROUPS, NB), jnp.float32, math.log(0.5), math.log(2.0))), 0.5, 2.0)
    obs_noise = centred(key_list[10], (BATCH_GROUPS, NB, MEMBERS), 1.0, 6.0, (), jnp.float32)
    return dict(ensemble=ensemble, northward_wind=northward_wind, eastward_wind=eastward_wind, spreading_strength=spreading_strength, measurement_home_subdomain=measurement_home_subdomain, obs_site=obs_site, obs_class=obs_class, cutoff_table=cutoff_table, obs_value=obs_value, obs_var=obs_var, obs_noise=obs_noise)


advect_coef = 0.2

def taper(dist, radius):
    z = dist / radius
    inner = 1.0 - 5.0 / 3.0 * z ** 2 + 0.625 * z ** 3 + 0.5 * z ** 4 - 0.25 * z ** 5
    outside = jnp.maximum(z, 1.0)
    outer = 4.0 - 5.0 * outside + 5.0 / 3.0 * outside ** 2 + 0.625 * outside ** 3 - 0.5 * outside ** 4 + outside ** 5 / 12.0 - 2.0 / (3.0 * outside)
    return jnp.where(z <= 1.0, inner, jnp.where(z < 2.0, outer, jnp.float32(0.0)))

def advance_subdomains(prognostic_fields, northward_wind, eastward_wind, spreading_strength):
    padded = jnp.pad(prognostic_fields, ((1, 1), (0, 0), (0, 0)))
    north = padded[2:]
    south = padded[:-2]
    east = jnp.roll(prognostic_fields, -1, axis=1)
    west = jnp.roll(prognostic_fields, 1, axis=1)
    lap = north + south + east + west - 4.0 * prognostic_fields
    return prognostic_fields + spreading_strength[:, :, None] * lap - advect_coef * (northward_wind[:, :, None] * (north - south) + eastward_wind[:, :, None] * (east - west))

def whiten(prior, value, var, noise):
    mean = lax.optimization_barrier(jnp.mean(prior, axis=1, keepdims=True))
    anom = prior - mean
    cov = jnp.dot(anom, anom.T, precision=lax.Precision.HIGHEST) / jnp.float32(MEMBERS - 1) + jnp.diag(var)
    factor = jnp.linalg.cholesky(cov)
    rhs = value[:, None] + jnp.sqrt(var)[:, None] * noise - prior
    return (anom, jax.scipy.linalg.cho_solve((factor, True), rhs))

def reference(ensemble, northward_wind, eastward_wind, spreading_strength, measurement_home_subdomain, obs_site, obs_class, cutoff_table, obs_value, obs_var, obs_noise):
    prognostic_fields = ensemble
    for section in range(SECTIONS):
        prognostic_fields = advance_subdomains(prognostic_fields, northward_wind, eastward_wind, spreading_strength)
    for k in range(BATCH_GROUPS):
        owner = measurement_home_subdomain[k].astype(jnp.int32)
        site = obs_site[k].astype(jnp.int32)
        cell = site // LEV
        level = site % LEV
        glat = owner // N_LON * CLAT + cell // CLON
        glon = owner % N_LON * CLON + cell % CLON
        grid = prognostic_fields.reshape(NLAT, NLON, LEV, MEMBERS)
        prior = grid[glat, glon, level]
        anom_obs, white = whiten(prior, obs_value[k], obs_var[k], obs_noise[k])
        radius = cutoff_table[obs_class[k]].astype(jnp.float32)
        vertical_profiles = jnp.arange(NLON, dtype=jnp.int32)

        def update(args):
            xrow, ilat = args
            dlat = jnp.abs(ilat - glat).astype(jnp.float32)
            dlon = jnp.abs(vertical_profiles[:, None] - glon[None, :])
            dlon = jnp.minimum(dlon, NLON - dlon).astype(jnp.float32)
            dist = jnp.sqrt(dlat[None, :] * dlat[None, :] + dlon * dlon)
            rho = taper(dist, radius[None, :])
            cube = xrow.reshape(NLON, LEV, MEMBERS)
            xp = cube - lax.optimization_barrier(jnp.mean(cube, axis=2, keepdims=True))
            cov = jnp.einsum('clm,jm->clj', xp, anom_obs, precision=lax.Precision.HIGHEST) / jnp.float32(MEMBERS - 1)
            inc = jnp.einsum('clj,jm->clm', cov * rho[:, None, :], white, precision=lax.Precision.HIGHEST)
            return (cube + inc).reshape(NLON, LEV * MEMBERS)
        prognostic_fields = lax.map(update, (prognostic_fields, jnp.arange(NLAT, dtype=jnp.int32)))
    return prognostic_fields
```

```python
import functools

import jax
import jax.numpy as jnp
from jax import lax
from jax.experimental import pallas as pl
from jax.experimental.pallas import tpu as pltpu
from jax.sharding import Mesh
from jax.sharding import PartitionSpec as P

LEV = 28
MEMBERS = 64
BATCH_GROUPS = 3
CAP = 4
NB = 512
CLAT = 4
CLON = 8
CELLS = CLAT * CLON
NLON = 256
N_LON = 32
WIDTH = LEV * MEMBERS
PACKED = WIDTH + 128
SLOTS = BATCH_GROUPS * CAP
ROWS = CELLS * LEV
OBS = BATCH_GROUPS * NB
HIGHEST = lax.Precision.HIGHEST
ADVECT = 0.2

LAT = ("x", "yl")
LON = ("z", "yh", "c")
PLANE = ("yl", "z", "yh")


def taper(dist, radius):
    z = dist / radius
    inner = 1.0 - 5.0 / 3.0 * z**2 + 0.625 * z**3 + 0.5 * z**4 - 0.25 * z**5
    outside = jnp.maximum(z, 1.0)
    outer = (
        4.0
        - 5.0 * outside
        + 5.0 / 3.0 * outside**2
        + 0.625 * outside**3
        - 0.5 * outside**4
        + outside**5 / 12.0
        - 2.0 / (3.0 * outside)
    )
    return jnp.where(z <= 1.0, inner, jnp.where(z < 2.0, outer, jnp.float32(0.0)))


def rho_of(lat_a, lon_a, lat_b, lon_b, radius_b):
    dlat = jnp.abs(lat_a[:, None] - lat_b[None, :]).astype(jnp.float32)
    dlon = jnp.abs(lon_a[:, None] - lon_b[None, :])
    dlon = jnp.minimum(dlon, NLON - dlon).astype(jnp.float32)
    dist = jnp.sqrt(dlat * dlat + dlon * dlon)
    return taper(dist, radius_b[None, :])


def forecast_kernel(site_ref, mid, lo, hi, west, east, x_ref, send_ref, grid, coef):
    grid[0:2, 0:8] = lo[...]
    grid[2:6, 0:8] = mid[...]
    grid[6:8, 0:8] = hi[...]
    grid[:, 8:16] = jnp.zeros((8, 8, PACKED), jnp.float32)
    grid[:, 8:10] = east[...]
    grid[:, 14:16] = west[...]
    winds = grid[1:7, :, WIDTH:PACKED]
    for n in range(3):
        coef[n] = jnp.broadcast_to(winds[:, :, n : n + 1], (6, 16, 128))

    def step(v, nw, ew, ss):
        here, north, south = v[1:-1], v[2:], v[:-2]
        east_of = pltpu.roll(here, 15, 1)
        west_of = pltpu.roll(here, 1, 1)
        lap = north + south + east_of + west_of - 4.0 * here
        return here + ss * lap - ADVECT * (nw * (north - south) + ew * (east_of - west_of))

    for chunk in range(WIDTH // 128):
        lanes = slice(chunk * 128, chunk * 128 + 128)
        first = step(grid[:, :, lanes], coef[0], coef[1], coef[2])
        second = step(first, coef[0, 1:5], coef[1, 1:5], coef[2, 1:5])
        x_ref[chunk] = second[:, 0:8].reshape(CELLS, 128)

    lane = lax.broadcasted_iota(jnp.int32, (1, 128), 1)
    for pair in range(SLOTS // 2):
        halves = []
        for half in range(2):
            site = site_ref[2 * pair + half]
            cell = site // LEV
            level = site - cell * LEV
            row = x_ref[level // 2, pl.ds(cell, 1), :]
            swap = (level % 2) != half
            halves.append(jnp.where(swap, pltpu.roll(row, 64, 1), row))
        both = jnp.where(lane < 64, halves[0], halves[1])
        send_ref[:, pair, :] = jnp.broadcast_to(both, (send_ref.shape[0], 128))
    send_ref[:, SLOTS // 2 :, :] = jnp.zeros((send_ref.shape[0], 2, 128), jnp.float32)


def forecast(sites, mid, lo, hi, west, east):
    vmem = pl.BlockSpec(memory_space=pltpu.VMEM)
    return pl.pallas_call(
        forecast_kernel,
        out_shape=(
            jax.ShapeDtypeStruct((WIDTH // 128, CELLS, 128), jnp.float32),
            jax.ShapeDtypeStruct((64, 8, 128), jnp.float32),
        ),
        in_specs=[pl.BlockSpec(memory_space=pltpu.SMEM)] + [vmem] * 5,
        out_specs=(vmem, vmem),
        scratch_shapes=[
            pltpu.VMEM((8, 16, PACKED), jnp.float32),
            pltpu.VMEM((3, 6, 16, 128), jnp.float32),
        ],
        compiler_params=pltpu.CompilerParams(vmem_limit_bytes=8 << 20),
        name="forecast",
    )(sites, mid, lo, hi, west, east)


def nt_dot(a, b):
    return lax.dot_general(
        a, b, (((1,), (1,)), ((), ())), precision=HIGHEST, preferred_element_type=jnp.float32
    )


def nn_dot(a, b):
    return lax.dot_general(
        a, b, (((1,), (0,)), ((), ())), precision=HIGHEST, preferred_element_type=jnp.float32
    )


def assimilate_kernel(
    row_ref, x_ref, mine, theirs, odd_ref, target_ref, rinv_ref, rho_obs, rho_own, out_ref, state, obs, every, rows_of
):
    every[0 : mine.shape[0], :] = mine[...]
    every[mine.shape[0] :, :] = theirs[...]

    @pl.loop(0, OBS // 16)
    def _(n):
        base = pl.multiple_of(n * 16, 16)
        for i in range(16):
            rows_of[pl.ds(base + i, 1), :] = every[pl.ds(row_ref[base + i], 1), :]

    picked = rows_of[...]
    obs[...] = jnp.where(odd_ref[...] > 0.5, picked[:, MEMBERS:], picked[:, :MEMBERS])
    for level in range(LEV):
        half = level % 2 * 64
        state[level * CELLS : (level + 1) * CELLS, :] = x_ref[level // 2, :, half : half + 64]
    row_id = lax.broadcasted_iota(jnp.int32, (MEMBERS, 1), 0)
    diag = lax.broadcasted_iota(jnp.int32, (MEMBERS, 128), 0) == lax.broadcasted_iota(
        jnp.int32, (MEMBERS, 128), 1
    )

    @pl.loop(0, BATCH_GROUPS)
    def _(k):
        here = pl.ds(pl.multiple_of(k * NB, NB), NB)
        prior = obs[here, :]
        anom = prior - jnp.mean(prior, axis=1, keepdims=True)
        rinv = rinv_ref[here, :]
        innovation = target_ref[here, :] - prior
        scaled = jnp.concatenate([anom * rinv, innovation * rinv], axis=1)
        work = nn_dot(anom.T, scaled)
        work = jnp.where(diag, work + jnp.float32(MEMBERS - 1), work)
        for p in range(MEMBERS):
            pivot = work[p : p + 1, :]
            factor = work[:, p : p + 1] * (1.0 / work[p : p + 1, p : p + 1])
            factor = jnp.where(row_id == p, 0.0, factor)
            work = work - factor * pivot
        pivots = jnp.sum(jnp.where(diag, work, 0.0), axis=1, keepdims=True)
        weights = work[:, MEMBERS:] / pivots
        white = (innovation - nn_dot(anom, weights)) * rinv * jnp.float32(1.0 / (MEMBERS - 1))

        def increment(block, rho):
            dev = block - jnp.mean(block, axis=1, keepdims=True)
            return nn_dot(nt_dot(dev, anom) * rho, white)

        @pl.loop(0, ROWS // 128)
        def _(n):
            rows = pl.ds(pl.multiple_of(n * 128, 128), 128)
            block = state[rows, :]
            rho = rho_own[k]
            state[rows, :] = block + increment(block, jnp.concatenate([rho] * 4, axis=0))

        @pl.loop((k + 1) * 4, BATCH_GROUPS * 4)
        def _(n):
            rows = pl.ds(pl.multiple_of(n * 128, 128), 128)
            from_rho = pl.ds(pl.multiple_of((n - 4 + 4 * k) * 128, 128), 128)
            block = obs[rows, :]
            obs[rows, :] = block + increment(block, rho_obs[from_rho, :])

    for level in range(0, LEV, 2):
        out_ref[:, level * 64 : level * 64 + 128] = jnp.concatenate(
            [state[level * CELLS : (level + 1) * CELLS, :], state[(level + 1) * CELLS : (level + 2) * CELLS, :]],
            axis=1,
        )


def assimilate(row, x, mine, theirs, odd, target, rinv, rho_obs, rho_own):
    vmem = pl.BlockSpec(memory_space=pltpu.VMEM)
    return pl.pallas_call(
        assimilate_kernel,
        out_shape=jax.ShapeDtypeStruct((CELLS, WIDTH), jnp.float32),
        in_specs=[pl.BlockSpec(memory_space=pltpu.SMEM)] + [vmem] * 8,
        out_specs=vmem,
        scratch_shapes=[
            pltpu.VMEM((ROWS, MEMBERS), jnp.float32),
            pltpu.VMEM((OBS, MEMBERS), jnp.float32),
            pltpu.VMEM((2 * 256 * SLOTS // 2, 128), jnp.float32),
            pltpu.VMEM((OBS, 128), jnp.float32),
        ],
        compiler_params=pltpu.CompilerParams(vmem_limit_bytes=24 << 20),
        name="assimilate",
    )(row, x, mine, theirs, odd, target, rinv, rho_obs, rho_own)


def plan(lat_tile, lon_tile, owner, site, obs_class, cutoff_table):
    cell = site // LEV
    glat = owner // N_LON * CLAT + cell // CLON
    glon = owner % N_LON * CLON + cell % CLON
    classes = jnp.arange(cutoff_table.shape[0], dtype=jnp.int32)
    match = (obs_class[:, :, None] == classes).astype(jnp.int32)
    radius = jnp.sum(match * cutoff_table, axis=2).astype(jnp.float32)
    order = jnp.arange(NB, dtype=jnp.int32)
    same = (owner[:, :, None] == owner[:, None, :]) & (order[None, :] < order[:, None])
    rank = jnp.sum(same.astype(jnp.int32), axis=2)
    slot = jnp.arange(BATCH_GROUPS, dtype=jnp.int32)[:, None] * CAP + rank
    mine = owner == lat_tile * N_LON + lon_tile
    chosen = mine[:, None, :] & (rank[:, None, :] == jnp.arange(CAP, dtype=jnp.int32)[:, None])
    sites = jnp.sum(jnp.where(chosen, site[:, None, :], 0), axis=2).reshape(SLOTS)
    lat, lon = owner // N_LON, owner % N_LON
    x, yl = lat // 4, lat % 4
    z, yh, c = lon // 4, lon // 2 % 2, lon % 2
    other = jnp.where(c == lon_tile % 2, 0, 1)
    row = (((other * 4 + x) * 64 + (yl * 8 + z) * 2 + yh) * (SLOTS // 2) + slot // 2).reshape(OBS)
    odd = jnp.broadcast_to((slot % 2).astype(jnp.float32).reshape(OBS, 1), (OBS, MEMBERS))
    rho_obs = jnp.concatenate(
        [
            rho_of(glat[1:].reshape(-1), glon[1:].reshape(-1), glat[0], glon[0], radius[0]),
            rho_of(glat[2], glon[2], glat[1], glon[1], radius[1]),
        ]
    )
    local = jnp.arange(CELLS, dtype=jnp.int32)
    cell_lat = lat_tile * CLAT + local // CLON
    cell_lon = lon_tile * CLON + local % CLON
    rho_own = jnp.stack(
        [rho_of(cell_lat, cell_lon, glat[k], glon[k], radius[k]) for k in range(BATCH_GROUPS)]
    )
    return sites, row, odd, rho_obs, rho_own


def halo(block, axes, count, dim, periodic):
    forward = [(i, i + 1) for i in range(count - 1)]
    if periodic:
        forward.append((count - 1, 0))
    backward = [(b, a) for a, b in forward]
    extent = block.shape[dim]
    low = lax.ppermute(lax.slice_in_dim(block, extent - 2, None, axis=dim), axes, forward)
    high = lax.ppermute(lax.slice_in_dim(block, 0, 2, axis=dim), axes, backward)
    return low, high


def body(
    ensemble,
    northward_wind,
    eastward_wind,
    spreading_strength,
    owner,
    site,
    obs_class,
    cutoff_table,
    obs_value,
    obs_var,
    obs_noise,
):
    lat_tile = lax.axis_index("x") * 4 + lax.axis_index("yl")
    lon_tile = lax.axis_index("z") * 4 + lax.axis_index("yh") * 2 + lax.axis_index("c")
    winds = jnp.stack([northward_wind, eastward_wind, spreading_strength], axis=2)
    winds = jnp.pad(winds, ((0, 0), (0, 0), (0, 125)))
    mid = jnp.concatenate([ensemble, winds], axis=2)
    lo, hi = halo(mid, LAT, 16, 0, False)
    tall = jnp.concatenate([lo, mid, hi], axis=0)
    west, east = halo(tall, LON, 32, 1, True)
    sites, row, odd, rho_obs, rho_own = plan(
        lat_tile, lon_tile, owner, site, obs_class, cutoff_table
    )
    target = (obs_value[:, :, None] + jnp.sqrt(obs_var)[:, :, None] * obs_noise).reshape(OBS, MEMBERS)
    rinv = jnp.broadcast_to((1.0 / obs_var).reshape(OBS, 1), (OBS, MEMBERS))
    state, send = forecast(sites, mid, lo, hi, west, east)
    plane = lax.all_to_all(send, PLANE, 0, 0)
    plane = plane[:, : SLOTS // 2, :].reshape(64 * SLOTS // 2, 128)
    cube = lax.all_to_all(jnp.broadcast_to(plane, (4,) + plane.shape), "x", 0, 0)
    cube = cube.reshape(-1, 128)
    partner = lax.ppermute(cube, "c", [(0, 1), (1, 0)])
    out = assimilate(row, state, cube, partner, odd, target, rinv, rho_obs, rho_own)
    return out.reshape(CLAT, CLON, WIDTH)


def solution(mesh):
    split = Mesh(mesh.devices.reshape(4, 4, 8, 2, 2), LAT + LON)
    tile = P(LAT, LON)
    return jax.shard_map(
        body,
        mesh=split,
        in_specs=(P(LAT, LON, None), tile, tile, tile) + (P(),) * 7,
        out_specs=P(LAT, LON, None),
        check_vma=False,
    )
```

```python
import functools

import jax
import jax.numpy as jnp
from jax import lax
from jax.experimental import pallas as pl
from jax.experimental.pallas import tpu as pltpu
from jax.sharding import Mesh
from jax.sharding import PartitionSpec as P

LEV = 28
MEMBERS = 64
BATCH_GROUPS = 3
CAP = 4
NB = 512
CLAT = 4
CLON = 8
CELLS = CLAT * CLON
NLON = 256
N_LON = 32
WIDTH = LEV * MEMBERS
PACKED = WIDTH + 128
SLOTS = BATCH_GROUPS * CAP
ROWS = CELLS * LEV
OBS = BATCH_GROUPS * NB
HIGHEST = lax.Precision.HIGHEST
ADVECT = 0.2

LAT = ("x", "yl")
LON = ("z", "yh", "c")
PLANE = ("yl", "z", "yh")


def taper(dist, radius):
    z = dist / radius
    inner = 1.0 - 5.0 / 3.0 * z**2 + 0.625 * z**3 + 0.5 * z**4 - 0.25 * z**5
    outside = jnp.maximum(z, 1.0)
    outer = (
        4.0
        - 5.0 * outside
        + 5.0 / 3.0 * outside**2
        + 0.625 * outside**3
        - 0.5 * outside**4
        + outside**5 / 12.0
        - 2.0 / (3.0 * outside)
    )
    return jnp.where(z <= 1.0, inner, jnp.where(z < 2.0, outer, jnp.float32(0.0)))


def rho_of(lat_a, lon_a, lat_b, lon_b, radius_b):
    dlat = jnp.abs(lat_a[:, None] - lat_b[None, :]).astype(jnp.float32)
    dlon = jnp.abs(lon_a[:, None] - lon_b[None, :])
    dlon = jnp.minimum(dlon, NLON - dlon).astype(jnp.float32)
    dist = jnp.sqrt(dlat * dlat + dlon * dlon)
    return taper(dist, radius_b[None, :])


def forecast_kernel(site_ref, mid, lo, hi, from_core, from_chip, x_ref, send_ref, grid, coef):
    grid[0:2, 0:8] = lo[...]
    grid[2:6, 0:8] = mid[...]
    grid[6:8, 0:8] = hi[...]
    grid[:, 8:16] = jnp.zeros((8, 8, PACKED), jnp.float32)
    second = site_ref[SLOTS] == 1
    grid[:, 8:10] = jnp.where(second, from_chip[...], from_core[...])
    grid[:, 14:16] = jnp.where(second, from_core[...], from_chip[...])
    winds = grid[1:7, :, WIDTH:PACKED]
    for n in range(3):
        coef[n] = jnp.broadcast_to(winds[:, :, n : n + 1], (6, 16, 128))

    def step(v, nw, ew, ss):
        here, north, south = v[1:-1], v[2:], v[:-2]
        east_of = pltpu.roll(here, 15, 1)
        west_of = pltpu.roll(here, 1, 1)
        lap = north + south + east_of + west_of - 4.0 * here
        return here + ss * lap - ADVECT * (nw * (north - south) + ew * (east_of - west_of))

    for chunk in range(WIDTH // 128):
        lanes = slice(chunk * 128, chunk * 128 + 128)
        first = step(grid[:, :, lanes], coef[0], coef[1], coef[2])
        second = step(first, coef[0, 1:5], coef[1, 1:5], coef[2, 1:5])
        x_ref[chunk] = second[:, 0:8].reshape(CELLS, 128)

    lane = lax.broadcasted_iota(jnp.int32, (1, 128), 1)
    for pair in range(SLOTS // 2):
        halves = []
        for half in range(2):
            site = site_ref[2 * pair + half]
            cell = site // LEV
            level = site - cell * LEV
            row = x_ref[level // 2, pl.ds(cell, 1), :]
            swap = (level % 2) != half
            halves.append(jnp.where(swap, pltpu.roll(row, 64, 1), row))
        both = jnp.where(lane < 64, halves[0], halves[1])
        send_ref[:, pair, :] = jnp.broadcast_to(both, (send_ref.shape[0], 128))
    send_ref[:, SLOTS // 2 :, :] = jnp.zeros((send_ref.shape[0], 2, 128), jnp.float32)


def forecast(sites, mid, lo, hi, from_core, from_chip):
    vmem = pl.BlockSpec(memory_space=pltpu.VMEM)
    return pl.pallas_call(
        forecast_kernel,
        out_shape=(
            jax.ShapeDtypeStruct((WIDTH // 128, CELLS, 128), jnp.float32),
            pltpu.VMEM((64, 8, 128), jnp.float32),
        ),
        in_specs=[pl.BlockSpec(memory_space=pltpu.SMEM)] + [vmem] * 5,
        out_specs=(vmem, vmem),
        scratch_shapes=[
            pltpu.VMEM((8, 16, PACKED), jnp.float32),
            pltpu.VMEM((3, 6, 16, 128), jnp.float32),
        ],
        compiler_params=pltpu.CompilerParams(vmem_limit_bytes=8 << 20),
        name="forecast",
    )(sites, mid, lo, hi, from_core, from_chip)


def full_dot(a, b):
    return lax.dot_general(
        a, b, (((1,), (0,)), ((), ())), precision=HIGHEST, preferred_element_type=jnp.float32
    )


def high(v):
    return v.astype(jnp.bfloat16).astype(jnp.float32)


def assimilate_kernel(
    row_ref, x_ref, mine, theirs, odd_ref, target_ref, rinv_ref, rho_one, rho_two, rho_own,
    out_ref, state, obs, every, rows_of, anom_split, white_split,
):
    left = lax.broadcasted_iota(jnp.int32, (1, 128), 1) < MEMBERS
    every[0 : mine.shape[0], :] = mine[...]
    every[mine.shape[0] :, :] = theirs[...]

    @pl.loop(0, OBS // 16)
    def _(n):
        base = pl.multiple_of(n * 16, 16)
        for i in range(16):
            rows_of[pl.ds(base + i, 1), :] = every[pl.ds(row_ref[base + i], 1), :]

    for level in range(0, LEV, 2):
        both = x_ref[level // 2]
        swapped = pltpu.roll(both, MEMBERS, 1)
        state[level * CELLS : (level + 1) * CELLS, :] = jnp.where(left, both, swapped)
        state[(level + 1) * CELLS : (level + 2) * CELLS, :] = jnp.where(left, swapped, both)
    picked = rows_of[...]
    swapped = pltpu.roll(picked, MEMBERS, 1)
    odd = odd_ref[...] > 0.5
    first = jnp.where(odd, swapped, picked)
    obs[...] = jnp.where(left, first, jnp.where(odd, picked, swapped))

    row_id = lax.broadcasted_iota(jnp.int32, (MEMBERS, 128), 0)
    lane_id = lax.broadcasted_iota(jnp.int32, (MEMBERS, 128), 1)
    diag = row_id == lane_id

    def centred(v):
        return v - jnp.sum(v, axis=1, keepdims=True) * jnp.float32(1.0 / 128)

    @pl.loop(0, BATCH_GROUPS)
    def _(k):
        here = pl.ds(pl.multiple_of(k * NB, NB), NB)
        prior = obs[here, :]
        anom = centred(prior)
        rinv = rinv_ref[here, :]
        innovation = target_ref[here, :] - prior
        anom_high = high(anom)
        anom_split[:, 0:128] = anom_high.astype(jnp.bfloat16)
        anom_split[:, 128:256] = (anom - anom_high).astype(jnp.bfloat16)
        work = full_dot(anom.T[:MEMBERS], jnp.where(left, anom, innovation) * rinv)
        work = jnp.where(diag, work + jnp.float32(MEMBERS - 1), work)
        for p in range(0, MEMBERS, 4):
            cols = [jnp.broadcast_to(work[:, p + t : p + t + 1], (MEMBERS, 128)) for t in range(4)]
            rows = [work[p + t : p + t + 1, :] for t in range(4)]
            e = [[cols[t][p + r : p + r + 1] for t in range(4)] for r in range(4)]
            det = 1.0 / (e[0][0] * e[1][1] - e[0][1] * e[1][0])
            top = [(e[1][1] * rows[0] - e[0][1] * rows[1]) * det, (e[0][0] * rows[1] - e[1][0] * rows[0]) * det]
            u = [[(e[1][1] * e[0][t] - e[0][1] * e[1][t]) * det for t in (2, 3)],
                 [(e[0][0] * e[1][t] - e[1][0] * e[0][t]) * det for t in (2, 3)]]
            s2 = [[e[r][t] - e[r][0] * u[0][t - 2] - e[r][1] * u[1][t - 2] for t in (2, 3)] for r in (2, 3)]
            low = [rows[r] - e[r][0] * top[0] - e[r][1] * top[1] for r in (2, 3)]
            det2 = 1.0 / (s2[0][0] * s2[1][1] - s2[0][1] * s2[1][0])
            new2 = (s2[1][1] * low[0] - s2[0][1] * low[1]) * det2
            new3 = (s2[0][0] * low[1] - s2[1][0] * low[0]) * det2
            new0 = top[0] - u[0][0] * new2 - u[0][1] * new3
            new1 = top[1] - u[1][0] * new2 - u[1][1] * new3
            new = [new0, new1, new2, new3]
            fresh = work
            for t in range(4):
                fresh = fresh - cols[t] * new[t]
            for t in range(4):
                fresh = jnp.where(row_id == p + t, new[t], fresh)
            work = fresh
        weights = jnp.where(left, pltpu.roll(work, MEMBERS, 1), work)
        white = innovation - full_dot(anom[:, :MEMBERS], weights)
        white = white * rinv * jnp.float32(1.0 / (MEMBERS - 1))
        white_high = high(white)
        white_split[...] = jnp.where(left, white_high, white - white_high).astype(jnp.bfloat16)

        def updated(block, rho):
            dev = centred(block)
            dev_high = high(dev)
            dev = jnp.where(left, dev_high, dev - dev_high).astype(jnp.bfloat16)
            cov = lax.dot_general(
                jnp.concatenate([dev, dev], axis=1),
                anom_split[...],
                (((1,), (1,)), ((), ())),
                preferred_element_type=jnp.float32,
            )
            cov = cov.reshape((-1,) + rho.shape) * rho
            cov = cov.reshape(-1, NB)
            cov_high = cov.astype(jnp.bfloat16)
            cov_low = (cov - cov_high.astype(jnp.float32)).astype(jnp.bfloat16)
            total = jnp.dot(cov_high, white_split[...], preferred_element_type=jnp.float32)
            total += jnp.dot(cov_low, white_split[...], preferred_element_type=jnp.float32)
            return block + (total + pltpu.roll(total, MEMBERS, 1))

        step = ROWS // 2

        @pl.loop(0, ROWS // step)
        def _(n):
            rows = pl.ds(pl.multiple_of(n * step, step), step)
            state[rows, :] = updated(state[rows, :], rho_own[k])

        def replay(first, rho):
            @pl.loop(0, rho.shape[0] // NB)
            def _(n):
                rows = pl.ds(pl.multiple_of(first + n * NB, NB), NB)
                from_rho = pl.ds(pl.multiple_of(n * NB, NB), NB)
                obs[rows, :] = updated(obs[rows, :], rho[from_rho, :])

        pl.when(k == 0)(lambda: replay(NB, rho_one))
        pl.when(k == 1)(lambda: replay(2 * NB, rho_two))

    for level in range(0, LEV, 2):
        low = state[level * CELLS : (level + 1) * CELLS, :]
        upper = state[(level + 1) * CELLS : (level + 2) * CELLS, :]
        out_ref[:, level * MEMBERS : (level + 2) * MEMBERS] = jnp.where(left, low, upper)


def assimilate(row, x, mine, theirs, odd, target, rinv, rho_one, rho_two, rho_own):
    vmem = pl.BlockSpec(memory_space=pltpu.VMEM)
    return pl.pallas_call(
        assimilate_kernel,
        out_shape=jax.ShapeDtypeStruct((CELLS, WIDTH), jnp.float32),
        in_specs=[pl.BlockSpec(memory_space=pltpu.SMEM)] + [vmem] * 9,
        out_specs=vmem,
        scratch_shapes=[
            pltpu.VMEM((ROWS, 128), jnp.float32),
            pltpu.VMEM((OBS, 128), jnp.float32),
            pltpu.VMEM((2 * 256 * SLOTS // 2, 128), jnp.float32),
            pltpu.VMEM((OBS, 128), jnp.float32),
            pltpu.VMEM((NB, 256), jnp.bfloat16),
            pltpu.VMEM((NB, 128), jnp.bfloat16),
        ],
        compiler_params=pltpu.CompilerParams(vmem_limit_bytes=24 << 20),
        name="assimilate",
    )(row, x, mine, theirs, odd, target, rinv, rho_one, rho_two, rho_own)


def slots(lat_tile, lon_tile, owner, site):
    order = jnp.arange(NB, dtype=jnp.int32)
    same = (owner[:, :, None] == owner[:, None, :]) & (order[None, :] < order[:, None])
    rank = jnp.sum(same.astype(jnp.int32), axis=2)
    slot = jnp.arange(BATCH_GROUPS, dtype=jnp.int32)[:, None] * CAP + rank
    mine = owner == lat_tile * N_LON + lon_tile
    chosen = mine[:, None, :] & (rank[:, None, :] == jnp.arange(CAP, dtype=jnp.int32)[:, None])
    sites = jnp.sum(jnp.where(chosen, site[:, None, :], 0), axis=2).reshape(SLOTS)
    lat, lon = owner // N_LON, owner % N_LON
    x, yl = lat // 4, lat % 4
    z, yh, c = lon // 4, lon // 2 % 2, lon % 2
    other = jnp.where(c == lon_tile % 2, 0, 1)
    row = ((other * 4 + x) * 64 + (yl * 8 + z) * 2 + yh) * (SLOTS // 2) + slot // 2
    return jnp.append(sites, lon_tile % 2), row.reshape(OBS), slot % 2


def tapers(lat_tile, lon_tile, owner, site, obs_class, cutoff_table):
    cell = site // LEV
    glat = owner // N_LON * CLAT + cell // CLON
    glon = owner % N_LON * CLON + cell % CLON
    classes = jnp.arange(cutoff_table.shape[0], dtype=jnp.int32)
    match = (obs_class[:, :, None] == classes).astype(jnp.int32)
    radius = jnp.sum(match * cutoff_table, axis=2).astype(jnp.float32)
    rho_one = rho_of(glat[1:].reshape(-1), glon[1:].reshape(-1), glat[0], glon[0], radius[0])
    rho_two = rho_of(glat[2], glon[2], glat[1], glon[1], radius[1])
    local = jnp.arange(CELLS, dtype=jnp.int32)
    cell_lat = lat_tile * CLAT + local // CLON
    cell_lon = lon_tile * CLON + local % CLON
    rho_own = jnp.stack(
        [rho_of(cell_lat, cell_lon, glat[k], glon[k], radius[k]) for k in range(BATCH_GROUPS)]
    )
    return rho_one, rho_two, rho_own


def lat_halo(block):
    forward = [(i, i + 1) for i in range(15)]
    backward = [(b, a) for a, b in forward]
    low = lax.ppermute(block[CLAT - 2 :], LAT, forward)
    high = lax.ppermute(block[:2], LAT, backward)
    return low, high


def lon_halo(block):
    second = lax.axis_index("c") == 1
    start, end = block[:, :2], block[:, CLON - 2 :]
    inner = jnp.where(second, start, end)
    outer = jnp.where(second, end, start)
    from_core = lax.ppermute(inner, "c", [(0, 1), (1, 0)])
    pairs = [(i, (i + 1) % N_LON) for i in range(1, N_LON, 2)]
    from_chip = lax.ppermute(outer, LON, pairs + [(b, a) for a, b in pairs])
    return from_core, from_chip


def body(
    ensemble,
    northward_wind,
    eastward_wind,
    spreading_strength,
    owner,
    site,
    obs_class,
    cutoff_table,
    obs_value,
    obs_var,
    obs_noise,
):
    lat_tile = lax.axis_index("x") * 4 + lax.axis_index("yl")
    lon_tile = lax.axis_index("z") * 4 + lax.axis_index("yh") * 2 + lax.axis_index("c")
    winds = jnp.stack([northward_wind, eastward_wind, spreading_strength], axis=2)
    winds = jnp.pad(winds, ((0, 0), (0, 0), (0, 125)))
    mid = jnp.concatenate([ensemble, winds], axis=2)
    lo, hi = lat_halo(mid)
    tall = jnp.concatenate([lo, mid, hi], axis=0)
    from_core, from_chip = lon_halo(tall)
    sites, row, parity = slots(lat_tile, lon_tile, owner, site)
    state, send = forecast(sites, mid, lo, hi, from_core, from_chip)
    send, parity, owner, site, obs_class, obs_var, obs_value, obs_noise = lax.optimization_barrier(
        (send, parity, owner, site, obs_class, obs_var, obs_value, obs_noise)
    )
    rho_one, rho_two, rho_own = tapers(lat_tile, lon_tile, owner, site, obs_class, cutoff_table)
    odd = jnp.broadcast_to(parity.astype(jnp.float32).reshape(OBS, 1), (OBS, 128))
    target = (obs_value[:, :, None] + jnp.sqrt(obs_var)[:, :, None] * obs_noise).reshape(OBS, MEMBERS)
    target = jnp.concatenate([target, target], axis=1)
    rinv = jnp.broadcast_to((1.0 / obs_var).reshape(OBS, 1), (OBS, 128))
    plane = lax.all_to_all(send, PLANE, 0, 0)
    plane = plane[:, : SLOTS // 2, :].reshape(64 * SLOTS // 2, 128)
    cube = lax.all_gather(plane, "x", tiled=True)
    partner = lax.ppermute(cube, "c", [(0, 1), (1, 0)])
    out = assimilate(row, state, cube, partner, odd, target, rinv, rho_one, rho_two, rho_own)
    return out.reshape(CLAT, CLON, WIDTH)


def solution(mesh):
    split = Mesh(mesh.devices.reshape(4, 4, 8, 2, 2), LAT + LON)
    tile = P(LAT, LON)
    return jax.shard_map(
        body,
        mesh=split,
        in_specs=(P(LAT, LON, None), tile, tile, tile) + (P(),) * 7,
        out_specs=P(LAT, LON, None),
        check_vma=False,
    )
```

```python
import functools

import jax
import jax.numpy as jnp
from jax import lax
from jax.experimental import pallas as pl
from jax.experimental.pallas import tpu as pltpu
from jax.sharding import Mesh
from jax.sharding import PartitionSpec as P

LEV = 28
MEMBERS = 64
BATCH_GROUPS = 3
CAP = 4
NB = 512
CLAT = 4
CLON = 8
CELLS = CLAT * CLON
NLON = 256
N_LON = 32
WIDTH = LEV * MEMBERS
PACKED = WIDTH + 128
SLOTS = BATCH_GROUPS * CAP
ROWS = CELLS * LEV
OBS = BATCH_GROUPS * NB
HIGHEST = lax.Precision.HIGHEST
ADVECT = 0.2
STEP = 224
EVERY = 4

LAT = ("x", "yl")
LON = ("z", "yh", "c")
PLANE = ("yl", "z", "yh")


def taper(dist, radius):
    z = dist / radius
    inner = 1.0 - 5.0 / 3.0 * z**2 + 0.625 * z**3 + 0.5 * z**4 - 0.25 * z**5
    outside = jnp.maximum(z, 1.0)
    outer = (
        4.0
        - 5.0 * outside
        + 5.0 / 3.0 * outside**2
        + 0.625 * outside**3
        - 0.5 * outside**4
        + outside**5 / 12.0
        - 2.0 / (3.0 * outside)
    )
    return jnp.where(z <= 1.0, inner, jnp.where(z < 2.0, outer, jnp.float32(0.0)))


def rho_of(lat_a, lon_a, lat_b, lon_b, radius_b):
    dlat = jnp.abs(lat_a[:, None] - lat_b[None, :]).astype(jnp.float32)
    dlon = jnp.abs(lon_a[:, None] - lon_b[None, :])
    dlon = jnp.minimum(dlon, NLON - dlon).astype(jnp.float32)
    dist = jnp.sqrt(dlat * dlat + dlon * dlon)
    return taper(dist, radius_b[None, :])


def forecast_kernel(site_ref, mid, lo, hi, from_core, from_chip, x_ref, send_ref, grid, coef):
    grid[0:2, 0:8] = lo[...]
    grid[2:6, 0:8] = mid[...]
    grid[6:8, 0:8] = hi[...]
    grid[:, 8:16] = jnp.zeros((8, 8, PACKED), jnp.float32)
    winds = grid[1:7, :, WIDTH:PACKED]
    for n in range(3):
        coef[n] = jnp.broadcast_to(winds[:, :, n : n + 1], (6, 16, 128))
    second = site_ref[SLOTS] == 1
    core, chip = from_core[...], from_chip[...]
    for near, far, edge in (
        (8, 9, jnp.where(second, chip, core)),
        (15, 14, jnp.where(second, core, chip)),
    ):
        grid[1:7, near : near + 1, 0:WIDTH] = edge[0:6]
        grid[2:6, far : far + 1, 0:WIDTH] = edge[6:10]
        for n in range(3):
            for r in range(CLAT):
                lane = n * CLAT + r
                coef[n, 1 + r, near : near + 1, :] = jnp.broadcast_to(edge[10, :, lane : lane + 1], (1, 128))

    def step(v, nw, ew, ss):
        here, north, south = v[1:-1], v[2:], v[:-2]
        east_of = pltpu.roll(here, 15, 1)
        west_of = pltpu.roll(here, 1, 1)
        lap = north + south + east_of + west_of - 4.0 * here
        return here + ss * lap - ADVECT * (nw * (north - south) + ew * (east_of - west_of))

    for chunk in range(WIDTH // 128):
        lanes = slice(chunk * 128, chunk * 128 + 128)
        first = step(grid[:, :, lanes], coef[0], coef[1], coef[2])
        second = step(first, coef[0, 1:5], coef[1, 1:5], coef[2, 1:5])
        x_ref[chunk] = second[:, 0:8].reshape(CELLS, 128)

    lane = lax.broadcasted_iota(jnp.int32, (1, 128), 1)
    for pair in range(SLOTS // 2):
        halves = []
        for half in range(2):
            site = site_ref[2 * pair + half]
            cell = site // LEV
            level = site - cell * LEV
            row = x_ref[level // 2, pl.ds(cell, 1), :]
            swap = (level % 2) != half
            halves.append(jnp.where(swap, pltpu.roll(row, 64, 1), row))
        both = jnp.where(lane < 64, halves[0], halves[1])
        send_ref[:, pair, :] = jnp.broadcast_to(both, (send_ref.shape[0], 128))
    send_ref[:, SLOTS // 2 :, :] = jnp.zeros((send_ref.shape[0], 2, 128), jnp.float32)


def forecast(sites, mid, lo, hi, from_core, from_chip):
    vmem = pl.BlockSpec(memory_space=pltpu.VMEM)
    return pl.pallas_call(
        forecast_kernel,
        out_shape=(
            jax.ShapeDtypeStruct((WIDTH // 128, CELLS, 128), jnp.float32),
            pltpu.VMEM((64, 8, 128), jnp.float32),
        ),
        in_specs=[pl.BlockSpec(memory_space=pltpu.SMEM)] + [vmem] * 5,
        out_specs=(vmem, vmem),
        scratch_shapes=[
            pltpu.VMEM((8, 16, PACKED), jnp.float32),
            pltpu.VMEM((3, 6, 16, 128), jnp.float32),
        ],
        compiler_params=pltpu.CompilerParams(vmem_limit_bytes=8 << 20),
        name="forecast",
    )(sites, mid, lo, hi, from_core, from_chip)


def high(v):
    return v.astype(jnp.bfloat16).astype(jnp.float32)


def assimilate_kernel(
    row_ref, x_ref, mine, theirs, target_ref, rinv_ref, rho_own, rho_one_hbm, rho_two_hbm,
    out_ref, state, obs, every, rho_one, rho_two, anom_split, white_split, sems,
):
    first_copy = pltpu.make_async_copy(rho_one_hbm, rho_one, sems.at[0])
    second_copy = pltpu.make_async_copy(rho_two_hbm, rho_two, sems.at[1])
    first_copy.start()
    second_copy.start()
    left = lax.broadcasted_iota(jnp.int32, (1, 128), 1) < MEMBERS
    pairs = mine.shape[0]
    for offset, part in ((0, mine), (pairs, theirs)):
        both = part[...]
        swapped = pltpu.roll(both, MEMBERS, 1)
        every[offset : offset + pairs, :] = jnp.where(left, both, swapped)
        every[2 * pairs + offset : 3 * pairs + offset, :] = jnp.where(left, swapped, both)

    @pl.loop(0, OBS // 16)
    def _(n):
        base = pl.multiple_of(n * 16, 16)
        for i in range(16):
            obs[pl.ds(base + i, 1), :] = every[pl.ds(row_ref[base + i], 1), :]

    for level in range(0, LEV, 2):
        both = x_ref[level // 2]
        swapped = pltpu.roll(both, MEMBERS, 1)
        state[level * CELLS : (level + 1) * CELLS, :] = jnp.where(left, both, swapped)
        state[(level + 1) * CELLS : (level + 2) * CELLS, :] = jnp.where(left, swapped, both)

    row_id = lax.broadcasted_iota(jnp.int32, (MEMBERS, 128), 0)
    lane_id = lax.broadcasted_iota(jnp.int32, (MEMBERS, 128), 1)

    def updated(block, rho, k):
        dev = block - jnp.sum(block, axis=1, keepdims=True) * jnp.float32(1.0 / 128)
        dev_high = high(dev)
        dev = jnp.where(left, dev_high, dev - dev_high).astype(jnp.bfloat16)
        cov = jnp.dot(
            jnp.concatenate([dev, dev], axis=1),
            anom_split[k],
            preferred_element_type=jnp.float32,
        )
        cov = (cov.reshape((-1,) + rho.shape) * rho).reshape(-1, NB)
        cov_high = cov.astype(jnp.bfloat16)
        cov_low = (cov - cov_high.astype(jnp.float32)).astype(jnp.bfloat16)
        total = sum(
            lax.dot_general(
                part,
                white_split[k],
                (((1,), (1,)), ((), ())),
                preferred_element_type=jnp.float32,
            )
            for part in (cov_high, cov_low)
        )
        return block + (total + pltpu.roll(total, MEMBERS, 1))

    def update_state(k, piece):
        rows = slice(piece * STEP, piece * STEP + STEP)
        state[rows, :] = updated(state[rows, :], rho_own[k], k)

    for k in range(BATCH_GROUPS):
        here = slice(k * NB, k * NB + NB)
        prior = obs[here, :].T[:MEMBERS]
        anom = prior - jnp.sum(prior, axis=0, keepdims=True) * jnp.float32(1.0 / MEMBERS)
        innovation = target_ref[k] - prior
        anom_high = high(anom)
        anom_low = anom - anom_high
        anom_split[k] = jnp.concatenate(
            [anom_high, anom_high, anom_low, anom_low], axis=0
        ).astype(jnp.bfloat16)
        work = lax.dot_general(
            anom * rinv_ref[k],
            jnp.concatenate([anom, innovation], axis=0),
            (((1,), (1,)), ((), ())),
            precision=HIGHEST,
            preferred_element_type=jnp.float32,
        )
        work = jnp.where(row_id == lane_id, work + jnp.float32(MEMBERS - 1), work)
        for p in range(0, MEMBERS, 4):
            if k and p % (4 * EVERY) == 0 and p // (4 * EVERY) < ROWS // STEP:
                update_state(k - 1, p // (4 * EVERY))
            cols = [jnp.broadcast_to(work[:, p + t : p + t + 1], (MEMBERS, 128)) for t in range(4)]
            rows = [work[p + t : p + t + 1, :] for t in range(4)]
            e = [[cols[t][p + r : p + r + 1] for t in range(4)] for r in range(4)]
            det = 1.0 / (e[0][0] * e[1][1] - e[0][1] * e[1][0])
            top0 = (e[1][1] * rows[0] - e[0][1] * rows[1]) * det
            top1 = (e[0][0] * rows[1] - e[1][0] * rows[0]) * det
            u0 = [(e[1][1] * e[0][t] - e[0][1] * e[1][t]) * det for t in (2, 3)]
            u1 = [(e[0][0] * e[1][t] - e[1][0] * e[0][t]) * det for t in (2, 3)]
            s = [[e[r][t] - e[r][0] * u0[t - 2] - e[r][1] * u1[t - 2] for t in (2, 3)] for r in (2, 3)]
            low = [rows[r] - e[r][0] * top0 - e[r][1] * top1 for r in (2, 3)]
            det = 1.0 / (s[0][0] * s[1][1] - s[0][1] * s[1][0])
            new2 = (s[1][1] * low[0] - s[0][1] * low[1]) * det
            new3 = (s[0][0] * low[1] - s[1][0] * low[0]) * det
            new0 = top0 - u0[0] * new2 - u0[1] * new3
            new1 = top1 - u1[0] * new2 - u1[1] * new3
            fresh = (new0, new1, new2, new3)
            for t in range(4):
                work = work - cols[t] * fresh[t]
            for t in range(4):
                work = jnp.where(row_id == p + t, fresh[t], work)
        weights = pltpu.roll(work, MEMBERS, 1)[:, :MEMBERS]
        white = innovation - lax.dot_general(
            weights,
            anom,
            (((0,), (0,)), ((), ())),
            precision=HIGHEST,
            preferred_element_type=jnp.float32,
        )
        white_high = high(white)
        white_split[k] = jnp.concatenate([white_high, white - white_high], axis=0).astype(jnp.bfloat16)

        if k < BATCH_GROUPS - 1:
            (first_copy, second_copy)[k].wait()
            rho = (rho_one, rho_two)[k]
            for n in range(BATCH_GROUPS - 1 - k):
                rows = slice((k + 1 + n) * NB, (k + 2 + n) * NB)
                obs[rows, :] = updated(obs[rows, :], rho[n * NB : n * NB + NB, :], k)
    for piece in range(ROWS // STEP):
        update_state(BATCH_GROUPS - 1, piece)

    for level in range(0, LEV, 2):
        low = state[level * CELLS : (level + 1) * CELLS, :]
        upper = state[(level + 1) * CELLS : (level + 2) * CELLS, :]
        out_ref[:, level * MEMBERS : (level + 2) * MEMBERS] = jnp.where(left, low, upper)


def assimilate(row, x, mine, theirs, target, rinv, rho_own, rho_one, rho_two):
    vmem = pl.BlockSpec(memory_space=pltpu.VMEM)
    hbm = pl.BlockSpec(memory_space=pltpu.HBM)
    return pl.pallas_call(
        assimilate_kernel,
        out_shape=jax.ShapeDtypeStruct((CELLS, WIDTH), jnp.float32),
        in_specs=[pl.BlockSpec(memory_space=pltpu.SMEM)] + [vmem] * 6 + [hbm] * 2,
        out_specs=vmem,
        scratch_shapes=[
            pltpu.VMEM((ROWS, 128), jnp.float32),
            pltpu.VMEM((OBS, 128), jnp.float32),
            pltpu.VMEM((4 * mine.shape[0], 128), jnp.float32),
            pltpu.VMEM(rho_one.shape, jnp.float32),
            pltpu.VMEM(rho_two.shape, jnp.float32),
            pltpu.VMEM((BATCH_GROUPS, 4 * MEMBERS, NB), jnp.bfloat16),
            pltpu.VMEM((BATCH_GROUPS, 2 * MEMBERS, NB), jnp.bfloat16),
            pltpu.SemaphoreType.DMA((2,)),
        ],
        compiler_params=pltpu.CompilerParams(vmem_limit_bytes=32 << 20),
        name="assimilate",
    )(row, x, mine, theirs, target, rinv, rho_own, rho_one, rho_two)


def slots(lat_tile, lon_tile, owner, site):
    order = jnp.arange(NB, dtype=jnp.int32)
    same = (owner[:, :, None] == owner[:, None, :]) & (order[None, :] < order[:, None])
    rank = jnp.sum(same.astype(jnp.int32), axis=2)
    slot = jnp.arange(BATCH_GROUPS, dtype=jnp.int32)[:, None] * CAP + rank
    mine = owner == lat_tile * N_LON + lon_tile
    chosen = mine[:, None, :] & (rank[:, None, :] == jnp.arange(CAP, dtype=jnp.int32)[:, None])
    sites = jnp.sum(jnp.where(chosen, site[:, None, :], 0), axis=2).reshape(SLOTS)
    lat, lon = owner // N_LON, owner % N_LON
    x, yl = lat // 4, lat % 4
    z, yh, c = lon // 4, lon // 2 % 2, lon % 2
    other = jnp.where(c == lon_tile % 2, 0, 1)
    row = ((other * 4 + x) * 64 + (yl * 8 + z) * 2 + yh) * (SLOTS // 2) + slot // 2
    row = row + slot % 2 * (N_LON * 16 * SLOTS // 2)
    return jnp.append(sites, lon_tile % 2), row.reshape(OBS)


def tapers(lat_tile, lon_tile, owner, site, obs_class, cutoff_table, scale):
    cell = site // LEV
    glat = owner // N_LON * CLAT + cell // CLON
    glon = owner % N_LON * CLON + cell % CLON
    classes = jnp.arange(cutoff_table.shape[0], dtype=jnp.int32)
    match = (obs_class[:, :, None] == classes).astype(jnp.int32)
    radius = jnp.sum(match * cutoff_table, axis=2).astype(jnp.float32)
    rho_one = rho_of(glat[1:].reshape(-1), glon[1:].reshape(-1), glat[0], glon[0], radius[0]) * scale[0]
    rho_two = rho_of(glat[2], glon[2], glat[1], glon[1], radius[1]) * scale[1]
    local = jnp.arange(CELLS, dtype=jnp.int32)
    cell_lat = lat_tile * CLAT + local // CLON
    cell_lon = lon_tile * CLON + local % CLON
    rho_own = jnp.stack(
        [rho_of(cell_lat, cell_lon, glat[k], glon[k], radius[k]) * scale[k] for k in range(BATCH_GROUPS)]
    )
    return rho_one, rho_two, rho_own


def lat_halo(block):
    forward = [(i, i + 1) for i in range(15)]
    backward = [(b, a) for a, b in forward]
    low = lax.ppermute(block[CLAT - 2 :], LAT, forward)
    high = lax.ppermute(block[:2], LAT, backward)
    return low, high


def lon_halo(lo, mid, hi, winds):
    def edge(near, far):
        fields = jnp.pad(winds[:, near].T.reshape(1, 3 * CLAT), ((0, 0), (0, WIDTH - 3 * CLAT)))
        parts = [lo[1:, near, :WIDTH], mid[:, near, :WIDTH], hi[:1, near, :WIDTH], mid[:, far, :WIDTH], fields]
        return jnp.concatenate(parts, axis=0)[:, None, :]

    second = lax.axis_index("c") == 1
    start, end = edge(0, 1), edge(CLON - 1, CLON - 2)
    inner = jnp.where(second, start, end)
    outer = jnp.where(second, end, start)
    from_core = lax.ppermute(inner, "c", [(0, 1), (1, 0)])
    pairs = [(i, (i + 1) % N_LON) for i in range(1, N_LON, 2)]
    from_chip = lax.ppermute(outer, LON, pairs + [(b, a) for a, b in pairs])
    return from_core, from_chip


def body(
    ensemble,
    northward_wind,
    eastward_wind,
    spreading_strength,
    owner,
    site,
    obs_class,
    cutoff_table,
    obs_value,
    obs_var,
    obs_noise,
):
    lat_tile = lax.axis_index("x") * 4 + lax.axis_index("yl")
    lon_tile = lax.axis_index("z") * 4 + lax.axis_index("yh") * 2 + lax.axis_index("c")
    winds = jnp.stack([northward_wind, eastward_wind, spreading_strength], axis=2)
    mid = jnp.concatenate([ensemble, jnp.pad(winds, ((0, 0), (0, 0), (0, 125)))], axis=2)
    lo, hi = lat_halo(mid)
    from_core, from_chip = lon_halo(lo, mid, hi, winds)
    sites, row = slots(lat_tile, lon_tile, owner, site)
    state, send = forecast(sites, mid, lo, hi, from_core, from_chip)
    send, owner, site, obs_class, obs_var, obs_value, obs_noise = lax.optimization_barrier(
        (send, owner, site, obs_class, obs_var, obs_value, obs_noise)
    )
    rinv = (1.0 / obs_var)[:, None, :]
    rho_one, rho_two, rho_own = tapers(
        lat_tile, lon_tile, owner, site, obs_class, cutoff_table, rinv / (MEMBERS - 1)
    )
    target = obs_value[:, None, :] + jnp.sqrt(obs_var)[:, None, :] * jnp.swapaxes(obs_noise, 1, 2)
    plane = lax.all_to_all(send, PLANE, 0, 0)
    plane = plane[:, : SLOTS // 2, :].reshape(64 * SLOTS // 2, 128)
    cube = lax.all_gather(plane, "x", tiled=True)
    partner = lax.ppermute(cube, "c", [(0, 1), (1, 0)])
    out = assimilate(row, state, cube, partner, target, rinv, rho_own, rho_one, rho_two)
    return out.reshape(CLAT, CLON, WIDTH)


def solution(mesh):
    split = Mesh(mesh.devices.reshape(4, 4, 8, 2, 2), LAT + LON)
    tile = P(LAT, LON)
    return jax.shard_map(
        body,
        mesh=split,
        in_specs=(P(LAT, LON, None), tile, tile, tile) + (P(),) * 7,
        out_specs=P(LAT, LON, None),
        check_vma=False,
    )
```

```python
import jax
import jax.numpy as jnp
from jax import lax
from jax.experimental import pallas as pl
from jax.experimental.pallas import tpu as pltpu
from jax.sharding import Mesh
from jax.sharding import PartitionSpec as P


LEV = 28
MEMBERS = 64
BATCH_GROUPS = 3
CAP = 4
NB = 512
CLAT = 4
CLON = 8
CELLS = CLAT * CLON
NLON = 256
N_LON = 32
WIDTH = LEV * MEMBERS
PACKED = WIDTH + 128
SLOTS = BATCH_GROUPS * CAP
ROWS = CELLS * LEV
OBS = BATCH_GROUPS * NB
HIGHEST = lax.Precision.HIGHEST
ADVECT = 0.2
STEP = 224
EVERY = 4

LAT = ("x", "yl")
LON = ("z", "yh", "c")
PLANE = ("yl", "z", "yh")


def taper(dist, radius):
    z = dist / radius
    inner = 1.0 - 5.0 / 3.0 * z**2 + 0.625 * z**3 + 0.5 * z**4 - 0.25 * z**5
    outside = jnp.maximum(z, 1.0)
    outer = (
        4.0
        - 5.0 * outside
        + 5.0 / 3.0 * outside**2
        + 0.625 * outside**3
        - 0.5 * outside**4
        + outside**5 / 12.0
        - 2.0 / (3.0 * outside)
    )
    return jnp.where(z <= 1.0, inner, jnp.where(z < 2.0, outer, jnp.float32(0.0)))


def rho_of(lat_a, lon_a, lat_b, lon_b, radius_b):
    dlat = jnp.abs(lat_a[:, None] - lat_b[None, :]).astype(jnp.float32)
    dlon = jnp.abs(lon_a[:, None] - lon_b[None, :])
    dlon = jnp.minimum(dlon, NLON - dlon).astype(jnp.float32)
    dist = jnp.sqrt(dlat * dlat + dlon * dlon)
    return taper(dist, radius_b[None, :])


def forecast_kernel(site_ref, mid, lo, hi, from_core, from_chip, x_ref, send_ref, grid, coef):
    grid[0:2, 0:8] = lo[...]
    grid[2:6, 0:8] = mid[...]
    grid[6:8, 0:8] = hi[...]
    winds = grid[1:7, :, WIDTH:PACKED]
    for n in range(3):
        coef[n] = jnp.broadcast_to(winds[:, :, n : n + 1], (6, 16, 128))
    second = site_ref[SLOTS] == 1
    core, chip = from_core[...], from_chip[...]
    for near, far, edge in (
        (8, 9, jnp.where(second, chip, core)),
        (15, 14, jnp.where(second, core, chip)),
    ):
        grid[1:7, near : near + 1, 0:WIDTH] = edge[0:6]
        grid[2:6, far : far + 1, 0:WIDTH] = edge[6:10]
        for n in range(3):
            for r in range(CLAT):
                lane = r * 128 + n
                coef[n, 1 + r, near : near + 1, :] = jnp.broadcast_to(edge[10, :, lane : lane + 1], (1, 128))

    def step(v, nw, ew, ss):
        here, north, south = v[1:-1], v[2:], v[:-2]
        east_of = pltpu.roll(here, 15, 1)
        west_of = pltpu.roll(here, 1, 1)
        lap = north + south + east_of + west_of - 4.0 * here
        return here + ss * lap - ADVECT * (nw * (north - south) + ew * (east_of - west_of))

    for chunk in range(WIDTH // 128):
        lanes = slice(chunk * 128, chunk * 128 + 128)
        first = step(grid[:, :, lanes], coef[0], coef[1], coef[2])
        second = step(first, coef[0, 1:5], coef[1, 1:5], coef[2, 1:5])
        x_ref[chunk] = second[:, 0:8].reshape(CELLS, 128)

    lane = lax.broadcasted_iota(jnp.int32, (1, 128), 1)
    for pair in range(SLOTS // 2):
        halves = []
        for half in range(2):
            site = site_ref[2 * pair + half]
            cell = site // LEV
            level = site - cell * LEV
            row = x_ref[level // 2, pl.ds(cell, 1), :]
            swap = (level % 2) != half
            halves.append(jnp.where(swap, pltpu.roll(row, 64, 1), row))
        both = jnp.where(lane < 64, halves[0], halves[1])
        send_ref[:, pair, :] = jnp.broadcast_to(both, (send_ref.shape[0], 128))
    send_ref[:, SLOTS // 2 :, :] = jnp.zeros((send_ref.shape[0], 2, 128), jnp.float32)


def forecast(sites, mid, lo, hi, from_core, from_chip):
    vmem = pl.BlockSpec(memory_space=pltpu.VMEM)
    return pl.pallas_call(
        forecast_kernel,
        out_shape=(
            jax.ShapeDtypeStruct((WIDTH // 128, CELLS, 128), jnp.float32),
            pltpu.VMEM((64, 8, 128), jnp.float32),
        ),
        in_specs=[pl.BlockSpec(memory_space=pltpu.SMEM)] + [vmem] * 5,
        out_specs=(vmem, vmem),
        scratch_shapes=[
            pltpu.VMEM((8, 16, PACKED), jnp.float32),
            pltpu.VMEM((3, 6, 16, 128), jnp.float32),
        ],
        compiler_params=pltpu.CompilerParams(vmem_limit_bytes=8 << 20),
        name="forecast",
    )(sites, mid, lo, hi, from_core, from_chip)


def high(v):
    return v.astype(jnp.bfloat16).astype(jnp.float32)


def assimilate_kernel(
    row_ref, x_ref, mine, theirs, target_ref, rinv_ref, rho_own, rho_one_hbm, rho_two_hbm,
    out_ref, state, obs, every, rho_one, rho_two, anom_split, white_split, sems,
):
    first_copy = pltpu.make_async_copy(rho_one_hbm, rho_one, sems.at[0])
    second_copy = pltpu.make_async_copy(rho_two_hbm, rho_two, sems.at[1])
    first_copy.start()
    second_copy.start()
    left = lax.broadcasted_iota(jnp.int32, (1, 128), 1) < MEMBERS
    pairs = mine.shape[0]
    for offset, part in ((0, mine), (pairs, theirs)):
        both = part[...]
        swapped = pltpu.roll(both, MEMBERS, 1)
        every[offset : offset + pairs, :] = jnp.where(left, both, swapped)
        every[2 * pairs + offset : 3 * pairs + offset, :] = jnp.where(left, swapped, both)

    @pl.loop(0, OBS // 16)
    def _(n):
        base = pl.multiple_of(n * 16, 16)
        for i in range(16):
            obs[pl.ds(base + i, 1), :] = every[pl.ds(row_ref[base + i], 1), :]

    for level in range(0, LEV, 2):
        both = x_ref[level // 2]
        swapped = pltpu.roll(both, MEMBERS, 1)
        state[level * CELLS : (level + 1) * CELLS, :] = jnp.where(left, both, swapped)
        state[(level + 1) * CELLS : (level + 2) * CELLS, :] = jnp.where(left, swapped, both)

    row_id = lax.broadcasted_iota(jnp.int32, (MEMBERS, 128), 0)
    lane_id = lax.broadcasted_iota(jnp.int32, (MEMBERS, 128), 1)

    def updated(block, rho, k):
        dev = block - jnp.sum(block, axis=1, keepdims=True) * jnp.float32(1.0 / 128)
        dev_high = high(dev)
        dev = jnp.where(left, dev_high, dev - dev_high).astype(jnp.bfloat16)
        cov = jnp.dot(
            jnp.concatenate([dev, dev], axis=1),
            anom_split[k],
            preferred_element_type=jnp.float32,
        )
        cov = (cov.reshape((-1,) + rho.shape) * rho).reshape(-1, NB)
        cov_high = cov.astype(jnp.bfloat16)
        cov_low = (cov - cov_high.astype(jnp.float32)).astype(jnp.bfloat16)
        total = sum(
            lax.dot_general(
                part,
                white_split[k],
                (((1,), (1,)), ((), ())),
                preferred_element_type=jnp.float32,
            )
            for part in (cov_high, cov_low)
        )
        return block + (total + pltpu.roll(total, MEMBERS, 1))

    def update_state(k, piece):
        rows = slice(piece * STEP, piece * STEP + STEP)
        state[rows, :] = updated(state[rows, :], rho_own[k], k)

    for k in range(BATCH_GROUPS):
        here = slice(k * NB, k * NB + NB)
        prior = obs[here, :].T[:MEMBERS]
        anom = prior - jnp.sum(prior, axis=0, keepdims=True) * jnp.float32(1.0 / MEMBERS)
        innovation = target_ref[k] - prior
        anom_high = high(anom)
        anom_low = anom - anom_high
        anom_split[k] = jnp.concatenate(
            [anom_high, anom_high, anom_low, anom_low], axis=0
        ).astype(jnp.bfloat16)
        work = lax.dot_general(
            anom * rinv_ref[k],
            jnp.concatenate([anom, innovation], axis=0),
            (((1,), (1,)), ((), ())),
            precision=HIGHEST,
            preferred_element_type=jnp.float32,
        )
        work = jnp.where(row_id == lane_id, work + jnp.float32(MEMBERS - 1), work)
        for p in range(0, MEMBERS, 4):
            if k and p % (4 * EVERY) == 0 and p // (4 * EVERY) < ROWS // STEP:
                update_state(k - 1, p // (4 * EVERY))
            cols = [jnp.broadcast_to(work[:, p + t : p + t + 1], (MEMBERS, 128)) for t in range(4)]
            rows = [work[p + t : p + t + 1, :] for t in range(4)]
            e = [[cols[t][p + r : p + r + 1] for t in range(4)] for r in range(4)]
            det = 1.0 / (e[0][0] * e[1][1] - e[0][1] * e[1][0])
            top0 = (e[1][1] * rows[0] - e[0][1] * rows[1]) * det
            top1 = (e[0][0] * rows[1] - e[1][0] * rows[0]) * det
            u0 = [(e[1][1] * e[0][t] - e[0][1] * e[1][t]) * det for t in (2, 3)]
            u1 = [(e[0][0] * e[1][t] - e[1][0] * e[0][t]) * det for t in (2, 3)]
            s = [[e[r][t] - e[r][0] * u0[t - 2] - e[r][1] * u1[t - 2] for t in (2, 3)] for r in (2, 3)]
            low = [rows[r] - e[r][0] * top0 - e[r][1] * top1 for r in (2, 3)]
            det = 1.0 / (s[0][0] * s[1][1] - s[0][1] * s[1][0])
            new2 = (s[1][1] * low[0] - s[0][1] * low[1]) * det
            new3 = (s[0][0] * low[1] - s[1][0] * low[0]) * det
            new0 = top0 - u0[0] * new2 - u0[1] * new3
            new1 = top1 - u1[0] * new2 - u1[1] * new3
            fresh = (new0, new1, new2, new3)
            for t in range(4):
                work = work - cols[t] * fresh[t]
            for t in range(4):
                work = jnp.where(row_id == p + t, fresh[t], work)
        weights = pltpu.roll(work, MEMBERS, 1)[:, :MEMBERS]
        white = innovation - lax.dot_general(
            weights,
            anom,
            (((0,), (0,)), ((), ())),
            precision=HIGHEST,
            preferred_element_type=jnp.float32,
        )
        white_high = high(white)
        white_split[k] = jnp.concatenate([white_high, white - white_high], axis=0).astype(jnp.bfloat16)

        if k < BATCH_GROUPS - 1:
            (first_copy, second_copy)[k].wait()
            rho = (rho_one, rho_two)[k]
            for n in range(BATCH_GROUPS - 1 - k):
                rows = slice((k + 1 + n) * NB, (k + 2 + n) * NB)
                obs[rows, :] = updated(obs[rows, :], rho[n * NB : n * NB + NB, :], k)
    for piece in range(ROWS // STEP):
        update_state(BATCH_GROUPS - 1, piece)

    for level in range(0, LEV, 2):
        low = state[level * CELLS : (level + 1) * CELLS, :]
        upper = state[(level + 1) * CELLS : (level + 2) * CELLS, :]
        out_ref[:, level * MEMBERS : (level + 2) * MEMBERS] = jnp.where(left, low, upper)


def assimilate(row, x, mine, theirs, target, rinv, rho_own, rho_one, rho_two):
    vmem = pl.BlockSpec(memory_space=pltpu.VMEM)
    hbm = pl.BlockSpec(memory_space=pltpu.HBM)
    return pl.pallas_call(
        assimilate_kernel,
        out_shape=jax.ShapeDtypeStruct((CELLS, WIDTH), jnp.float32),
        in_specs=[pl.BlockSpec(memory_space=pltpu.SMEM)] + [vmem] * 6 + [hbm] * 2,
        out_specs=vmem,
        scratch_shapes=[
            pltpu.VMEM((ROWS, 128), jnp.float32),
            pltpu.VMEM((OBS, 128), jnp.float32),
            pltpu.VMEM((4 * mine.shape[0], 128), jnp.float32),
            pltpu.VMEM(rho_one.shape, jnp.float32),
            pltpu.VMEM(rho_two.shape, jnp.float32),
            pltpu.VMEM((BATCH_GROUPS, 4 * MEMBERS, NB), jnp.bfloat16),
            pltpu.VMEM((BATCH_GROUPS, 2 * MEMBERS, NB), jnp.bfloat16),
            pltpu.SemaphoreType.DMA((2,)),
        ],
        compiler_params=pltpu.CompilerParams(vmem_limit_bytes=32 << 20),
        name="assimilate",
    )(row, x, mine, theirs, target, rinv, rho_own, rho_one, rho_two)


def slots(lat_tile, lon_tile, owner, site):
    order = jnp.arange(NB, dtype=jnp.int32)
    same = (owner[:, :, None] == owner[:, None, :]) & (order[None, :] < order[:, None])
    rank = jnp.sum(same.astype(jnp.int32), axis=2)
    slot = jnp.arange(BATCH_GROUPS, dtype=jnp.int32)[:, None] * CAP + rank
    mine = owner == lat_tile * N_LON + lon_tile
    chosen = mine[:, None, :] & (rank[:, None, :] == jnp.arange(CAP, dtype=jnp.int32)[:, None])
    sites = jnp.sum(jnp.where(chosen, site[:, None, :], 0), axis=2).reshape(SLOTS)
    lat, lon = owner // N_LON, owner % N_LON
    x, yl = lat // 4, lat % 4
    z, yh, c = lon // 4, lon // 2 % 2, lon % 2
    other = jnp.where(c == lon_tile % 2, 0, 1)
    row = ((other * 4 + x) * 64 + (yl * 8 + z) * 2 + yh) * (SLOTS // 2) + slot // 2
    row = row + slot % 2 * (N_LON * 16 * SLOTS // 2)
    return jnp.append(sites, lon_tile % 2), row.reshape(OBS)


def tapers(lat_tile, lon_tile, owner, site, obs_class, cutoff_table, scale):
    cell = site // LEV
    glat = owner // N_LON * CLAT + cell // CLON
    glon = owner % N_LON * CLON + cell % CLON
    classes = jnp.arange(cutoff_table.shape[0], dtype=jnp.int32)
    match = (obs_class[:, :, None] == classes).astype(jnp.int32)
    radius = jnp.sum(match * cutoff_table, axis=2).astype(jnp.float32)
    rho_one = rho_of(glat[1:].reshape(-1), glon[1:].reshape(-1), glat[0], glon[0], radius[0]) * scale[0]
    rho_two = rho_of(glat[2], glon[2], glat[1], glon[1], radius[1]) * scale[1]
    local = jnp.arange(CELLS, dtype=jnp.int32)
    cell_lat = lat_tile * CLAT + local // CLON
    cell_lon = lon_tile * CLON + local % CLON
    rho_own = jnp.stack(
        [rho_of(cell_lat, cell_lon, glat[k], glon[k], radius[k]) * scale[k] for k in range(BATCH_GROUPS)]
    )
    return rho_one, rho_two, rho_own


def lat_halo(block):
    forward = [(i, i + 1) for i in range(15)]
    backward = [(b, a) for a, b in forward]
    low = lax.ppermute(block[CLAT - 2 :], LAT, forward)
    high = lax.ppermute(block[:2], LAT, backward)
    return low, high


def edges_kernel(core_ref, lo, mid, hi, inner, outer):
    second = core_ref[0] == 1

    def put(row, pick):
        start, end = pick(0), pick(CLON - 1)
        lanes = slice(0, start.shape[1])
        inner[row, :, lanes] = jnp.where(second, start, end)
        outer[row, :, lanes] = jnp.where(second, end, start)

    put(0, lambda c: lo[1, c : c + 1, 0:WIDTH])
    put(5, lambda c: hi[0, c : c + 1, 0:WIDTH])
    for r in range(CLAT):
        put(1 + r, lambda c: mid[r, c : c + 1, 0:WIDTH])
        put(6 + r, lambda c: mid[r, abs(c - 1) : abs(c - 1) + 1, 0:WIDTH])
    put(10, lambda c: jnp.concatenate([mid[r, c : c + 1, WIDTH:PACKED] for r in range(CLAT)], axis=1))
    rest = slice(CLAT * 128, WIDTH)
    inner[10, :, rest] = jnp.zeros((1, WIDTH - CLAT * 128), jnp.float32)
    outer[10, :, rest] = jnp.zeros((1, WIDTH - CLAT * 128), jnp.float32)


def edges(core, lo, mid, hi):
    vmem = pl.BlockSpec(memory_space=pltpu.VMEM)
    return pl.pallas_call(
        edges_kernel,
        out_shape=(jax.ShapeDtypeStruct((11, 1, WIDTH), jnp.float32),) * 2,
        in_specs=[pl.BlockSpec(memory_space=pltpu.SMEM)] + [vmem] * 3,
        out_specs=(vmem, vmem),
        compiler_params=pltpu.CompilerParams(vmem_limit_bytes=8 << 20),
        name="edges",
    )(core, lo, mid, hi)


def lon_halo(inner, outer):
    pairs = [(i, (i + 1) % N_LON) for i in range(1, N_LON, 2)]
    from_chip = lax.ppermute(outer, LON, pairs + [(b, a) for a, b in pairs])
    from_core = lax.ppermute(inner, "c", [(0, 1), (1, 0)])
    return from_core, from_chip


def body(
    ensemble,
    northward_wind,
    eastward_wind,
    spreading_strength,
    owner,
    site,
    obs_class,
    cutoff_table,
    obs_value,
    obs_var,
    obs_noise,
):
    lat_tile = lax.axis_index("x") * 4 + lax.axis_index("yl")
    lon_tile = lax.axis_index("z") * 4 + lax.axis_index("yh") * 2 + lax.axis_index("c")
    winds = jnp.stack([northward_wind, eastward_wind, spreading_strength], axis=2)
    mid = jnp.concatenate([ensemble, jnp.pad(winds, ((0, 0), (0, 0), (0, 125)))], axis=2)
    lo, hi = lat_halo(mid)
    inner, outer = edges(lax.axis_index("c").astype(jnp.int32).reshape(1), lo, mid, hi)
    from_core, from_chip = lon_halo(inner, outer)
    sites, row = slots(lat_tile, lon_tile, owner, site)
    state, send = forecast(sites, mid, lo, hi, from_core, from_chip)
    send, owner, site, obs_class, obs_var, obs_value, obs_noise = lax.optimization_barrier(
        (send, owner, site, obs_class, obs_var, obs_value, obs_noise)
    )
    rinv = (1.0 / obs_var)[:, None, :]
    rho_one, rho_two, rho_own = tapers(
        lat_tile, lon_tile, owner, site, obs_class, cutoff_table, rinv / (MEMBERS - 1)
    )
    target = obs_value[:, None, :] + jnp.sqrt(obs_var)[:, None, :] * jnp.swapaxes(obs_noise, 1, 2)
    plane = lax.all_to_all(send, PLANE, 0, 0)
    plane = plane[:, : SLOTS // 2, :].reshape(64 * SLOTS // 2, 128)
    cube = lax.all_gather(plane, "x", tiled=True)
    partner = lax.ppermute(cube, "c", [(0, 1), (1, 0)])
    out = assimilate(row, state, cube, partner, target, rinv, rho_own, rho_one, rho_two)
    return out.reshape(CLAT, CLON, WIDTH)


def solution(mesh):
    split = Mesh(mesh.devices.reshape(4, 4, 8, 2, 2), LAT + LON)
    tile = P(LAT, LON)
    return jax.shard_map(
        body,
        mesh=split,
        in_specs=(P(LAT, LON, None), tile, tile, tile) + (P(),) * 7,
        out_specs=P(LAT, LON, None),
        check_vma=False,
    )
```
